128 devices in a mesh: space: 32 (over y, z, core), tm: 4 (over x).
Axes of the slice: x: 4, y: 4, z: 4, core: 2. Of those that a mesh axis runs over, the one named last changes fastest.
Arguments:
- field: float32 [32768, 8192], P('space', 'tm'), may hold values from -6 to 6
- range_test: float32 [8192, 256], P('tm'), may hold values from -0.0625 to 0.0625
- corange_test: float32 [512, 32768], P(None, 'space'), may hold values from -0.03125 to 0.03125
Outputs:
- left_factor: float32 [32768, 256], P('space')
- right_factor: float32 [256, 8192], P(None, 'tm')
- residual: float32 [32768, 8192], P('space', 'tm')
The draws below stay inside these ranges and needn't reach their ends.
All inputs are finite; a program needn't handle non-finite values.
Results may differ from the reference program's by a relative error of at most 0.00017.
Values sent between devices are 32-bit elements; how exact they have to be, the bound alone decides.
A program may use at most 128 MiB of HBM per device.

```python
import jax
import jax.numpy as jnp
from jax import lax

RANK = 256
CORANGE = 512
CELLS = 32768
TIMES = 8192


def block_levels(rng, dims, pieces, low, largest):
    factor_of = 1.0
    for dim, parts in pieces:
        steps = jax.random.uniform(jax.random.fold_in(jax.random.fold_in(rng, 6), dim), (parts,), jnp.float32, low / len(pieces), largest / len(pieces))
        factor_of = factor_of * jnp.repeat(jnp.exp(steps), dims[dim] // parts).reshape((-1,) + (1,) * (len(dims) - 1 - dim))
    return factor_of


def scatter_about(rng, shape, spread, reach, shards=(), kind=jnp.bfloat16):
    values = jax.random.normal(rng, shape, jnp.float32) * spread
    if len(shards) > 0:
        values = block_levels(rng, shape, shards, -0.22, 0.18) * values
    return jnp.clip(values, min=-reach, max=reach).astype(kind)


def setup_inputs(seed: int = 0) -> dict:
    splits = jax.random.split(jax.random.key(seed), 4)
    field = scatter_about(splits[0], (CELLS, TIMES), 1.0, 6.0, ((0, 32), (1, 4)), jnp.float32)
    range_test = scatter_about(splits[1], (TIMES, RANK), TIMES ** -0.5, 0.0625, ((0, 4),), jnp.float32)
    corange_test = scatter_about(splits[2], (CORANGE, CELLS), CELLS ** -0.5, 0.03125, ((1, 32),), jnp.float32)
    return dict(field=field, range_test=range_test, corange_test=corange_test)


def product(left, right):
    return jnp.dot(left.astype(jnp.float32), right.astype(jnp.float32), preferred_element_type=jnp.float32, precision=lax.Precision.HIGHEST)

def reference(field, range_test, corange_test):
    sketch = product(field, range_test)
    cosketch = product(corange_test, field)
    gram = product(sketch.T, sketch)
    lower = jnp.linalg.cholesky(gram)
    basis = lax.linalg.triangular_solve(lower, sketch, left_side=False, lower=True, transpose_a=True)
    core = product(corange_test, basis)
    normal = product(core.T, core)
    factor = jnp.linalg.cholesky(normal)
    rhs = product(core.T, cosketch)
    middle = lax.linalg.triangular_solve(factor, rhs, left_side=True, lower=True)
    right_factor = lax.linalg.triangular_solve(factor, middle, left_side=True, lower=True, transpose_a=True)
    residual = field - product(basis, right_factor)
    left_factor = basis * jnp.sqrt(jnp.float32(CELLS))
    return (left_factor, right_factor, residual)
```

```python
import functools

import jax
import jax.numpy as jnp
from jax import lax
from jax.experimental import pallas as pl
from jax.experimental.pallas import tpu as pltpu
from jax.sharding import PartitionSpec as P

MESH = pl.DeviceIdType.MESH
F32, BF16 = jnp.float32, jnp.bfloat16
HI = lax.Precision.HIGHEST


def halves(x):
    high = x.astype(BF16)
    return high, (x - high.astype(F32)).astype(BF16)


def mm(a, b):
    return jnp.dot(a, b, preferred_element_type=F32)


def mm3(ah, al, bh, bl):
    return mm(ah, bh) + (mm(ah, bl) + mm(al, bh))


def exact(a, b):
    return jnp.dot(a, b, preferred_element_type=F32, precision=HI)


def eliminate(matrix):
    lane = lax.broadcasted_iota(jnp.int32, (8, 128), 1)
    sub = lax.broadcasted_iota(jnp.int32, (8, 128), 0)

    def group(g, blocks):
        old = blocks
        blocks = list(blocks)
        for i in range(8):
            at = lane == i
            pivot = blocks[0]
            col = jnp.broadcast_to(pivot[:, i : i + 1], (8, 128))
            inv = 1.0 / jnp.broadcast_to(col[i : i + 1, :], (8, 128))
            row = jnp.broadcast_to(pivot[i : i + 1, :], (8, 128))
            row = jnp.where(at, 1.0, row) * inv
            below = sub > i
            blocks[0] = jnp.where(below, jnp.where(at, 0.0, pivot) - col * row, pivot)
            for b in range(1, 16):
                blk = blocks[b]
                c = jnp.broadcast_to(blk[:, i : i + 1], (8, 128))
                blocks[b] = jnp.where(at, 0.0, blk) - c * row
        for b in range(1, 16):
            blocks[b] = jnp.where(b < 16 - g, blocks[b], old[b])
        blocks = [pltpu.roll(x, 120, 1) for x in blocks]
        return tuple(blocks[1:] + blocks[:1])

    blocks = tuple(matrix[8 * b : 8 * b + 8, :] for b in range(16))
    blocks = lax.fori_loop(0, 16, group, blocks)
    full = jnp.concatenate(blocks, axis=0)
    r = lax.broadcasted_iota(jnp.int32, (128, 128), 0)
    c = lax.broadcasted_iota(jnp.int32, (128, 128), 1)
    diag = jnp.sum(jnp.where(r == c, full, 0.0), axis=1, keepdims=True)
    scale = 1.0 / jnp.sqrt(diag)
    upper = jnp.where(c >= r, full, 0.0) * scale
    lower = jnp.where(c < r, full, jnp.where(c == r, 1.0, 0.0)) * scale
    return upper, lower


def kernel(
    field, rng, cor, s_out, x_out, j_out, r_out,
    fbuf, rbuf, obuf, fh, fl, rh, rl, oh, ol,
    part, precv, sbuf,
    cpart, crecv, c1a, c1b, h2a, h2b, c2a, c2b, cfin,
    m_part, m_r0, m_h1, m_r1, m_h2, m_r2, m_r3, m_fin,
    g_part, g_r0, g_h1, g_r1, g_h2, g_r2, g_r3, g_fin,
    xbuf, jbuf, rfac,
    lsem, ssem, rsem, csend, crecvs,
):
    x = lax.axis_index("tm")
    sp = lax.axis_index("space")
    core = lax.rem(sp, 2)
    z = lax.rem(sp // 2, 4)
    y = sp // 8
    oc = 1 - core

    def plus(v, d):
        return lax.rem(v + d, 4)

    def to_core():
        return {"space": sp + 1 - 2 * core}

    def to_z(zz):
        return {"space": y * 8 + zz * 2 + core}

    def to_y(yy):
        return {"space": yy * 8 + z * 2 + core}

    def to_x(xx):
        return {"tm": xx}

    def al(v, n):
        return pl.multiple_of(v, n)

    count = [0]
    sent = []

    def send(src, dst, peer):
        i = count[0]
        count[0] += 1
        copy = pltpu.make_async_remote_copy(
            src_ref=src, dst_ref=dst, send_sem=ssem.at[i], recv_sem=rsem.at[i],
            device_id=peer, device_id_type=MESH)
        copy.start()
        sent.append(copy)
        return copy

    loads = [pltpu.make_async_copy(rng, rbuf, lsem.at[0])]
    order = (2, 1, 3, 0)
    for n, d in enumerate(order):
        rows = pl.ds(al(plus(x, d) * 256, 256), 256)
        loads.append(pltpu.make_async_copy(field.at[rows], fbuf.at[rows], lsem.at[1 + n]))
    loads.append(pltpu.make_async_copy(cor, obuf, lsem.at[5]))
    for load in loads:
        load.start()

    barrier = pltpu.get_barrier_semaphore()
    peers = [to_core()]
    for d in (1, 2, 3):
        peers += [to_z(plus(z, d)), to_y(plus(y, d)), to_x(plus(x, d))]
    for peer in peers:
        pl.semaphore_signal(barrier, inc=1, device_id=peer, device_id_type=MESH)
    pl.semaphore_wait(barrier, len(peers))

    def all_reduce(w, part, r0, h1, r1, h2, r2, r3, fin):
        base = al(core * 256, 256)
        cp = send(part.at[pl.ds(al(oc * 256, 256), 256)], r0, to_core())
        yield
        cp.wait_recv()
        h1[...] = part[pl.ds(base, 256), :] + r0[...]
        cps = []
        for d in (1, 2, 3):
            zz, yy = plus(z, d), plus(y, d)
            cps.append(send(h1.at[pl.ds(al(32 * zz, 32), 32)], r1.at[0, d - 1], to_z(zz)))
            cps.append(send(h1.at[pl.ds(al(128 + 32 * yy, 32), 32)], r1.at[1, d - 1], to_y(yy)))
        yield
        for cp in cps:
            cp.wait_recv()
        for k, v in ((0, z), (1, y)):
            h2[k] = (h1[pl.ds(al(128 * k + 32 * v, 32), 32), :] + r1[k, 0]) + (r1[k, 1] + r1[k, 2])
        cps = []
        for d in (1, 2, 3):
            zz, yy = plus(z, d), plus(y, d)
            cps.append(send(h2.at[0, pl.ds(al(8 * yy, 8), 8)], r2.at[0, d - 1], to_y(yy)))
            cps.append(send(h2.at[1, pl.ds(al(8 * zz, 8), 8)], r2.at[1, d - 1], to_z(zz)))
        yield
        for cp in cps:
            cp.wait_recv()
        for k, v in ((0, y), (1, z)):
            r3[x, 8 * k : 8 * k + 8, :] = (h2[k, pl.ds(al(8 * v, 8), 8), :] + r2[k, 0]) + (r2[k, 1] + r2[k, 2])
        cps = [send(r3.at[x], r3.at[x], to_x(plus(x, d))) for d in (1, 2, 3)]
        yield
        for cp in cps:
            cp.wait_recv()
        total = (r3[0] + r3[1]) + (r3[2] + r3[3])
        a = al(base + 32 * z, 32)
        b = al(base + 128 + 32 * y, 32)
        a8 = pl.ds(al(a + 8 * y, 8), 8)
        b8 = pl.ds(al(b + 8 * z, 8), 8)
        fin[a8, :] = total[0:8]
        fin[b8, :] = total[8:16]
        cps = []
        for d in (1, 2, 3):
            cps.append(send(fin.at[a8], fin.at[a8], to_y(plus(y, d))))
            cps.append(send(fin.at[b8], fin.at[b8], to_z(plus(z, d))))
        yield
        for cp in cps:
            cp.wait_recv()
        a32, b32 = pl.ds(a, 32), pl.ds(b, 32)
        cps = []
        for d in (1, 2, 3):
            cps.append(send(fin.at[a32], fin.at[a32], to_z(plus(z, d))))
            cps.append(send(fin.at[b32], fin.at[b32], to_y(plus(y, d))))
        yield
        for cp in cps:
            cp.wait_recv()
        mine = pl.ds(base, 256)
        cp = send(fin.at[mine], fin.at[mine], to_core())
        yield
        cp.wait_recv()
        yield

    loads[0].wait()
    high, low = halves(rbuf[...])
    rh[...] = high
    rl[...] = low
    pcopies = []
    for n, d in enumerate(order):
        loads[1 + n].wait()
        xx = plus(x, d)
        rows = pl.ds(al(xx * 256, 256), 256)
        high, low = halves(fbuf[rows, :])
        fh[rows, :] = high
        fl[rows, :] = low
        part[rows, :] = mm3(fh[rows, :], fl[rows, :], rh[...], rl[...])
        if d:
            pcopies.append(send(part.at[rows], precv.at[d - 1], to_x(xx)))

    loads[5].wait()
    high, low = halves(obuf[...])
    oh[...] = high
    ol[...] = low
    high, low = halves(part[...])
    m_part[...] = mm3(oh[...], ol[...], high, low)
    ar_m = all_reduce(256, m_part, m_r0, m_h1, m_r1, m_h2, m_r2, m_r3, m_fin)
    next(ar_m)

    other = pl.ds(al(oc * 256, 256), 256)
    mine = pl.ds(al(core * 256, 256), 256)

    def core_copy(j):
        yy, zz = j // 2, lax.rem(j, 2) * 2
        pair = pl.ds(zz, 2)
        return pltpu.make_async_remote_copy(
            src_ref=cpart.at[yy, pair, other], dst_ref=crecv.at[yy, pair],
            send_sem=csend.at[j], recv_sem=crecvs.at[j], device_id=to_core(), device_id_type=MESH)

    def cos_step(j, carry):
        cols = pl.ds(al(j * 256, 256), 256)
        block = mm3(oh[...], ol[...], fh[:, cols], fl[:, cols])
        yy, zz = j // 2, lax.rem(j, 2) * 2
        cpart[yy, zz] = block[:, :128]
        cpart[yy, zz + 1] = block[:, 128:]
        core_copy(j).start()
        return carry

    def cos_join(j, carry):
        core_copy(j).wait_recv()
        yy, zz = j // 2, lax.rem(j, 2) * 2
        pair = pl.ds(zz, 2)
        crecv[yy, pair] = crecv[yy, pair] + cpart[yy, pair, mine]
        return carry

    lax.fori_loop(0, 2, cos_step, 0)
    next(ar_m)
    lax.fori_loop(2, 4, cos_step, 0)
    next(ar_m)
    lax.fori_loop(4, 6, cos_step, 0)
    next(ar_m)
    for cp in pcopies:
        cp.wait_recv()
    own = pl.ds(al(x * 256, 256), 256)
    rows_sum = (part[own, :] + precv[0]) + (precv[1] + precv[2])
    sbuf[own, :] = rows_sum
    scopies = [send(sbuf.at[own], sbuf.at[own], to_x(plus(x, d))) for d in (1, 2, 3)]
    gram = exact(rows_sum.T, rows_sum)
    g_part[0:256, :] = gram[:, :128]
    g_part[256:512, :] = gram[:, 128:]
    ar_g = all_reduce(128, g_part, g_r0, g_h1, g_r1, g_h2, g_r2, g_r3, g_fin)
    next(ar_g)
    next(ar_m)
    lax.fori_loop(6, 8, cos_step, 0)
    next(ar_g)
    next(ar_m)
    lax.fori_loop(0, 8, cos_join, 0)
    c1 = []
    for d in (1, 2, 3):
        zz, yy = plus(z, d), plus(y, d)
        c1.append(send(crecv.at[:, zz, 0:128], c1a.at[d - 1], to_z(zz)))
        c1.append(send(crecv.at[yy, :, 128:256], c1b.at[d - 1], to_y(yy)))
    next(ar_g)
    next(ar_m)
    next(ar_m)
    mixed = m_fin[...]
    mixed_t = mixed.T
    normal = exact(mixed_t, mixed)

    def factor_first(a):
        up, lo = eliminate(a[:128, :128])
        off = exact(lo, a[:128, 128:])
        return up, lo, off, a[128:, 128:] - exact(off.T, off)

    def factor_second(up, lo, off, rest):
        up2, lo2 = eliminate(rest)
        corner = -exact(lo2, exact(off.T, lo))
        zero = jnp.zeros((128, 128), F32)
        left = jnp.concatenate([lo, corner], axis=0)
        right = jnp.concatenate([zero, lo2], axis=0)
        inv = jnp.concatenate([left, right], axis=1)
        top = jnp.concatenate([up, off], axis=1)
        bottom = jnp.concatenate([zero, up2], axis=1)
        return inv, jnp.concatenate([top, bottom], axis=0)

    next(ar_g)
    first = factor_first(normal)
    next(ar_g)
    for cp in c1:
        cp.wait_recv()
    for n in range(4):
        h2a[n] = (crecv[n, z, 0:128, :] + c1a[0, n]) + (c1a[1, n] + c1a[2, n])
        h2b[n] = (crecv[y, n, 128:256, :] + c1b[0, n]) + (c1b[1, n] + c1b[2, n])
    c2 = []
    for d in (1, 2, 3):
        zz, yy = plus(z, d), plus(y, d)
        c2.append(send(h2a.at[yy], c2a.at[d - 1], to_y(yy)))
        c2.append(send(h2b.at[zz], c2b.at[d - 1], to_z(zz)))
    inverse, unused = factor_second(*first)
    next(ar_g)
    for cp in c2:
        cp.wait_recv()
    cbase = al(core * 256, 256)
    cfin[pl.ds(cbase, 128), :] = (h2a[y] + c2a[0]) + (c2a[1] + c2a[2])
    cfin[pl.ds(al(cbase + 128, 128), 128), :] = (h2b[z] + c2b[0]) + (c2b[1] + c2b[2])
    cc = send(cfin.at[mine], cfin.at[mine], to_core())
    solve = exact(inverse.T, exact(inverse, mixed_t))
    cc.wait_recv()
    block = exact(solve, cfin[...])
    half = al(core * 128, 128)
    jbuf[...] = block
    ra = pl.ds(half, 64)
    rb = pl.ds(al(half + 64, 64), 64)
    xbuf[y, z, ra] = jbuf[ra, :]
    xbuf[y, z, rb] = jbuf[rb, :]
    x1 = []
    for d in (1, 2, 3):
        x1.append(send(xbuf.at[y, z, ra], xbuf.at[y, z, ra], to_z(plus(z, d))))
        x1.append(send(xbuf.at[y, z, rb], xbuf.at[y, z, rb], to_y(plus(y, d))))
    next(ar_g)
    next(ar_g)
    for cp in scopies:
        cp.wait_recv()
    outs = [pltpu.make_async_copy(sbuf, s_out, lsem.at[6])]
    outs[0].start()
    gram = jnp.concatenate([g_fin[0:256, :], g_fin[256:512, :]], axis=1)
    for cp in x1:
        cp.wait_recv()
    x2, forward = [], []
    for d in (1, 2, 3):
        x2.append(send(xbuf.at[y, :, ra], xbuf.at[y, :, ra], to_y(plus(y, d))))
        x2.append(send(xbuf.at[:, z, rb], xbuf.at[:, z, rb], to_z(plus(z, d))))
    forward.append(send(xbuf.at[y, :, ra], xbuf.at[y, :, ra], to_core()))
    forward.append(send(xbuf.at[:, z, rb], xbuf.at[:, z, rb], to_core()))
    first = factor_first(gram)
    for d, (ca, cb) in zip((1, 2, 3), zip(x2[0::2], x2[1::2])):
        ca.wait_recv()
        cb.wait_recv()
        yy, zz = plus(y, 4 - d), plus(z, 4 - d)
        forward.append(send(xbuf.at[yy, :, ra], xbuf.at[yy, :, ra], to_core()))
        forward.append(send(xbuf.at[:, zz, rb], xbuf.at[:, zz, rb], to_core()))
    inverse, upper = factor_second(*first)
    jbuf2, rfac2 = jbuf, rfac
    rfac2[0] = inverse
    rfac2[1] = upper
    for cp in forward:
        cp.wait_recv()
    outs.append(pltpu.make_async_copy(xbuf, x_out, lsem.at[7]))
    outs.append(pltpu.make_async_copy(rfac.at[0], j_out, lsem.at[8]))
    outs.append(pltpu.make_async_copy(rfac.at[1], r_out, lsem.at[9]))
    for copy in outs[1:]:
        copy.start()
    for cp in sent:
        cp.wait_send()

    def drain(j, carry):
        core_copy(j).wait_send()
        return carry

    lax.fori_loop(0, 8, drain, 0)
    for copy in outs:
        copy.wait()


def last(scale, field, s, xb, inv, up, left, right, residual, sh, sl):
    @pl.when(pl.program_id(0) == 0)
    def _():
        high, low = halves(s[...])
        sh[...] = high
        sl[...] = low

    j = pl.program_id(0)
    block = jnp.concatenate([xb[0], xb[1]], axis=1)
    xh, xl = halves(block)
    residual[...] = field[...] - mm3(sh[...], sl[...], xh, xl)
    uh, ul = halves(up[...])
    right[...] = mm3(uh, ul, xh, xl)
    ih, il = halves(inv[...].T)
    rows = pl.ds(pl.multiple_of(j * 128, 128), 128)
    left[...] = mm3(sh[rows, :], sl[rows, :], ih, il) * scale


def per_device(cells, field, range_test, corange_test):
    def vm(*shape, dtype=F32):
        return pltpu.VMEM(shape, dtype)

    def reduce_buffers(w):
        return [
            vm(512, w), vm(256, w), vm(256, w), vm(2, 3, 32, w), vm(2, 32, w),
            vm(2, 3, 8, w), vm(4, 16, w), vm(512, w),
        ]

    any_space = pl.BlockSpec(memory_space=pl.ANY)
    s, xb, inv, up = pl.pallas_call(
        kernel,
        out_shape=(
            jax.ShapeDtypeStruct((1024, 256), F32),
            jax.ShapeDtypeStruct((4, 4, 256, 128), F32),
            jax.ShapeDtypeStruct((256, 256), F32),
            jax.ShapeDtypeStruct((256, 256), F32),
        ),
        in_specs=[any_space] * 3,
        out_specs=[any_space] * 4,
        scratch_shapes=[
            vm(1024, 2048), vm(2048, 256), vm(512, 1024),
            vm(1024, 2048, dtype=BF16), vm(1024, 2048, dtype=BF16),
            vm(2048, 256, dtype=BF16), vm(2048, 256, dtype=BF16),
            vm(512, 1024, dtype=BF16), vm(512, 1024, dtype=BF16),
            vm(1024, 256), vm(3, 256, 256), vm(1024, 256),
            vm(4, 4, 512, 128), vm(4, 4, 256, 128),
            vm(3, 4, 128, 128), vm(3, 4, 128, 128), vm(4, 128, 128), vm(4, 128, 128),
            vm(3, 128, 128), vm(3, 128, 128), vm(512, 128),
            *reduce_buffers(256),
            *reduce_buffers(128),
            vm(4, 4, 256, 128), vm(256, 128), vm(2, 256, 256),
            pltpu.SemaphoreType.DMA((10,)),
            pltpu.SemaphoreType.DMA((120,)),
            pltpu.SemaphoreType.DMA((120,)),
            pltpu.SemaphoreType.DMA((8,)),
            pltpu.SemaphoreType.DMA((8,)),
        ],
        compiler_params=pltpu.CompilerParams(
            collective_id=0, has_side_effects=True, vmem_limit_bytes=64 * 1024 * 1024 - 65536),
        name="sketch",
    )(field, range_test, corange_test)
    xb = xb.reshape(16, 256, 128)
    return pl.pallas_call(
        functools.partial(last, float(cells) ** 0.5),
        grid=(8,),
        out_shape=(
            jax.ShapeDtypeStruct((1024, 256), F32),
            jax.ShapeDtypeStruct((256, 2048), F32),
            jax.ShapeDtypeStruct((1024, 2048), F32),
        ),
        in_specs=[
            pl.BlockSpec((1024, 256), lambda j: (0, j)),
            pl.BlockSpec((1024, 256), lambda j: (0, 0)),
            pl.BlockSpec((2, 256, 128), lambda j: (j, 0, 0)),
            pl.BlockSpec((256, 256), lambda j: (0, 0)),
            pl.BlockSpec((256, 256), lambda j: (0, 0)),
        ],
        out_specs=(
            pl.BlockSpec((128, 256), lambda j: (j, 0)),
            pl.BlockSpec((256, 256), lambda j: (0, j)),
            pl.BlockSpec((1024, 256), lambda j: (0, j)),
        ),
        scratch_shapes=[vm(1024, 256, dtype=BF16), vm(1024, 256, dtype=BF16)],
        name="finish",
    )(field, s, xb, inv, up)


def solution(mesh):
    cells = 1024 * mesh.shape["space"]
    return jax.shard_map(
        functools.partial(per_device, cells),
        mesh=mesh,
        in_specs=(P("space", "tm"), P("tm", None), P(None, "space")),
        out_specs=(P("space", None), P(None, "tm"), P("space", "tm")),
        check_vma=False,
    )
```

```python
import functools

import jax
import jax.numpy as jnp
from jax import lax
from jax.experimental import pallas as pl
from jax.experimental.pallas import tpu as pltpu
from jax.sharding import PartitionSpec as P

MESH = pl.DeviceIdType.MESH
F32, BF16 = jnp.float32, jnp.bfloat16
HI = lax.Precision.HIGHEST


def halves(x):
    high = x.astype(BF16)
    return high, (x - high.astype(F32)).astype(BF16)


def mm(a, b):
    return jnp.dot(a, b, preferred_element_type=F32)


def mm3(ah, al, bh, bl):
    return mm(ah, bh) + (mm(ah, bl) + mm(al, bh))


def exact(a, b):
    return jnp.dot(a, b, preferred_element_type=F32, precision=HI)


def eliminate(matrix):
    lane = lax.broadcasted_iota(jnp.int32, (8, 128), 1)
    sub = lax.broadcasted_iota(jnp.int32, (8, 128), 0)

    def spread(v, index):
        return jnp.take_along_axis(v, index, axis=1, mode="promise_in_bounds")

    def level(v, i):
        return jnp.broadcast_to(v[i : i + 1, :], (8, 128))

    def tree(terms):
        while len(terms) > 1:
            terms = [terms[k] + terms[k + 1] for k in range(0, len(terms), 2)]
        return terms[0]

    def group(active, g, carry):
        before, *blocks = carry
        index = [jnp.full((8, 128), 8 * g + i, jnp.int32) for i in range(8)]
        past = [jnp.maximum(v - 8, 0) for v in index]
        inside_past = (lane >= 8 * g - 8) & (lane < 8 * g)
        inside = (lane >= 8 * g) & (lane < 8 * g + 8)
        w = kept = blocks[0]
        cols = [spread(w, k) for k in index]
        old_rows = [level(before, i) for i in range(8)]
        out = {b: jnp.where(inside_past, 0.0, blocks[b]) for b in range(1, active + 1)}
        first = [spread(blocks[1], past[i]) * old_rows[i] for i in range(8)]
        out[1] = out[1] - tree(first)
        ahead = [spread(out[1], k) for k in index]
        for i in range(8):
            at = lane == index[i]
            inv = 1.0 / level(cols[i], i)
            row = jnp.where(at, 1.0, level(w, i))
            mine = sub == i
            kept = jnp.where(mine, w, kept)
            w = jnp.where(mine, row * inv, jnp.where(at, 0.0, w) - (cols[i] * row) * inv)
            for m in range(i + 1, 8):
                r = level(cols[m], i)
                cols[m] = jnp.where(mine, r * inv, cols[m] - (cols[i] * r) * inv)
            for b in range(2, active + 1):
                out[b] = out[b] - spread(blocks[b], past[i]) * old_rows[i]
        new = list(blocks)
        for b in range(2, active + 1):
            new[b] = jnp.where(b < 16 - g, out[b], blocks[b])
        pivot = jnp.where(inside, 0.0, out[1]) - tree([ahead[i] * level(w, i) for i in range(8)])
        new[1] = jnp.where(g < 15, pivot, blocks[1])
        return (w, *new[1:], kept)

    carry = (jnp.zeros((8, 128), F32), *(matrix[8 * b : 8 * b + 8, :] for b in range(16)))
    for n, active in enumerate((15, 11, 7, 3)):
        carry = lax.fori_loop(4 * n, 4 * n + 4, functools.partial(group, active), carry)
    full = jnp.concatenate(carry[1:], axis=0)
    r = lax.broadcasted_iota(jnp.int32, (128, 128), 0)
    c = lax.broadcasted_iota(jnp.int32, (128, 128), 1)
    diag = jnp.sum(jnp.where(r == c, full, 0.0), axis=1, keepdims=True)
    scale = 1.0 / jnp.sqrt(diag)
    upper = jnp.where(c >= r, full, 0.0) * scale
    lower = jnp.where(c < r, full, jnp.where(c == r, 1.0, 0.0)) * scale
    return upper, lower


def kernel(
    field, rng, cor, fbuf, sbuf, xbuf, j_out, r_out,
    rbuf, obuf, fh, fl, rh, rl, oh, ol,
    part, precv,
    cpart, crecv, c1a, c1b, h2a, h2b, c2a, c2b, cfin,
    m_part, m_r0, m_h1, m_r1, m_h2, m_r2, m_r3, m_fin,
    g_part, g_r0, g_h1, g_r1, g_h2, g_r2, g_r3, g_fin,
    jbuf,
    lsem, ssem, rsem, csend, crecvs,
):
    x = lax.axis_index("tm")
    sp = lax.axis_index("space")
    core = lax.rem(sp, 2)
    z = lax.rem(sp // 2, 4)
    y = sp // 8
    oc = 1 - core

    def plus(v, d):
        return lax.rem(v + d, 4)

    def to_core():
        return {"space": sp + 1 - 2 * core}

    def to_z(zz):
        return {"space": y * 8 + zz * 2 + core}

    def to_y(yy):
        return {"space": yy * 8 + z * 2 + core}

    def to_x(xx):
        return {"tm": xx}

    def al(v, n):
        return pl.multiple_of(v, n)

    count = [0]
    sent = []

    def send(src, dst, peer):
        i = count[0]
        count[0] += 1
        copy = pltpu.make_async_remote_copy(
            src_ref=src, dst_ref=dst, send_sem=ssem.at[i], recv_sem=rsem.at[i],
            device_id=peer, device_id_type=MESH)
        copy.start()
        sent.append(copy)
        return copy

    loads = [pltpu.make_async_copy(rng, rbuf, lsem.at[0])]
    order = (2, 1, 3, 0)
    for n, d in enumerate(order):
        rows = pl.ds(al(plus(x, d) * 256, 256), 256)
        loads.append(pltpu.make_async_copy(field.at[rows], fbuf.at[rows], lsem.at[1 + n]))
    loads.append(pltpu.make_async_copy(cor, obuf, lsem.at[5]))
    for load in loads:
        load.start()

    barrier = pltpu.get_barrier_semaphore()
    peers = [to_core()]
    for d in (1, 2, 3):
        peers += [to_z(plus(z, d)), to_y(plus(y, d)), to_x(plus(x, d))]
    for peer in peers:
        pl.semaphore_signal(barrier, inc=1, device_id=peer, device_id_type=MESH)

    def all_reduce(w, part, r0, h1, r1, h2, r2, r3, fin):
        base = al(core * 256, 256)
        cp = send(part.at[pl.ds(al(oc * 256, 256), 256)], r0, to_core())
        yield
        cp.wait_recv()
        h1[...] = part[pl.ds(base, 256), :] + r0[...]
        cps = []
        for d in (1, 2, 3):
            zz, yy = plus(z, d), plus(y, d)
            cps.append(send(h1.at[pl.ds(al(32 * zz, 32), 32)], r1.at[0, d - 1], to_z(zz)))
            cps.append(send(h1.at[pl.ds(al(128 + 32 * yy, 32), 32)], r1.at[1, d - 1], to_y(yy)))
        yield
        for cp in cps:
            cp.wait_recv()
        for k, v in ((0, z), (1, y)):
            h2[k] = (h1[pl.ds(al(128 * k + 32 * v, 32), 32), :] + r1[k, 0]) + (r1[k, 1] + r1[k, 2])
        cps = []
        for d in (1, 2, 3):
            zz, yy = plus(z, d), plus(y, d)
            cps.append(send(h2.at[0, pl.ds(al(8 * yy, 8), 8)], r2.at[0, d - 1], to_y(yy)))
            cps.append(send(h2.at[1, pl.ds(al(8 * zz, 8), 8)], r2.at[1, d - 1], to_z(zz)))
        yield
        for cp in cps:
            cp.wait_recv()
        for k, v in ((0, y), (1, z)):
            r3[x, 8 * k : 8 * k + 8, :] = (h2[k, pl.ds(al(8 * v, 8), 8), :] + r2[k, 0]) + (r2[k, 1] + r2[k, 2])
        cps = [send(r3.at[x], r3.at[x], to_x(plus(x, d))) for d in (1, 2, 3)]
        yield
        for cp in cps:
            cp.wait_recv()
        total = (r3[0] + r3[1]) + (r3[2] + r3[3])
        a = al(base + 32 * z, 32)
        b = al(base + 128 + 32 * y, 32)
        a8 = pl.ds(al(a + 8 * y, 8), 8)
        b8 = pl.ds(al(b + 8 * z, 8), 8)
        fin[a8, :] = total[0:8]
        fin[b8, :] = total[8:16]
        cps = []
        for d in (1, 2, 3):
            cps.append(send(fin.at[a8], fin.at[a8], to_y(plus(y, d))))
            cps.append(send(fin.at[b8], fin.at[b8], to_z(plus(z, d))))
        yield
        for cp in cps:
            cp.wait_recv()
        a32, b32 = pl.ds(a, 32), pl.ds(b, 32)
        cps = []
        for d in (1, 2, 3):
            cps.append(send(fin.at[a32], fin.at[a32], to_z(plus(z, d))))
            cps.append(send(fin.at[b32], fin.at[b32], to_y(plus(y, d))))
        yield
        for cp in cps:
            cp.wait_recv()
        mine = pl.ds(base, 256)
        cp = send(fin.at[mine], fin.at[mine], to_core())
        yield
        cp.wait_recv()
        yield

    loads[0].wait()
    high, low = halves(rbuf[...])
    rh[...] = high
    rl[...] = low
    pcopies = []
    for n, d in enumerate(order):
        loads[1 + n].wait()
        xx = plus(x, d)
        rows = pl.ds(al(xx * 256, 256), 256)
        high, low = halves(fbuf[rows, :])
        fh[rows, :] = high
        fl[rows, :] = low
        part[rows, :] = mm3(fh[rows, :], fl[rows, :], rh[...], rl[...])
        if n == 0:
            pl.semaphore_wait(barrier, len(peers))
        if d:
            pcopies.append(send(part.at[rows], precv.at[d - 1], to_x(xx)))

    loads[5].wait()
    high, low = halves(obuf[...])
    oh[...] = high
    ol[...] = low
    high, low = halves(part[...])
    m_part[...] = mm3(oh[...], ol[...], high, low)
    ar_m = all_reduce(256, m_part, m_r0, m_h1, m_r1, m_h2, m_r2, m_r3, m_fin)
    next(ar_m)

    other = pl.ds(al(oc * 256, 256), 256)
    mine = pl.ds(al(core * 256, 256), 256)

    def core_copy(j):
        yy, zz = j // 2, lax.rem(j, 2) * 2
        pair = pl.ds(zz, 2)
        return pltpu.make_async_remote_copy(
            src_ref=cpart.at[yy, pair, other], dst_ref=crecv.at[yy, pair],
            send_sem=csend.at[j], recv_sem=crecvs.at[j], device_id=to_core(), device_id_type=MESH)

    def cos_step(j, carry):
        cols = pl.ds(al(j * 256, 256), 256)
        block = mm3(oh[...], ol[...], fh[:, cols], fl[:, cols])
        yy, zz = j // 2, lax.rem(j, 2) * 2
        cpart[yy, zz] = block[:, :128]
        cpart[yy, zz + 1] = block[:, 128:]
        core_copy(j).start()
        return carry

    def cos_join(j, carry):
        core_copy(j).wait_recv()
        yy, zz = j // 2, lax.rem(j, 2) * 2
        pair = pl.ds(zz, 2)
        crecv[yy, pair] = crecv[yy, pair] + cpart[yy, pair, mine]
        return carry

    lax.fori_loop(0, 2, cos_step, 0)
    next(ar_m)
    lax.fori_loop(2, 4, cos_step, 0)
    next(ar_m)
    lax.fori_loop(4, 6, cos_step, 0)
    next(ar_m)
    for cp in pcopies:
        cp.wait_recv()
    own = pl.ds(al(x * 256, 256), 256)
    rows_sum = (part[own, :] + precv[0]) + (precv[1] + precv[2])
    sbuf[own, :] = rows_sum
    scopies = [send(sbuf.at[own], sbuf.at[own], to_x(plus(x, d))) for d in (1, 2, 3)]
    gram = exact(rows_sum.T, rows_sum)
    g_part[0:256, :] = gram[:, :128]
    g_part[256:512, :] = gram[:, 128:]
    ar_g = all_reduce(128, g_part, g_r0, g_h1, g_r1, g_h2, g_r2, g_r3, g_fin)
    next(ar_g)
    next(ar_m)
    lax.fori_loop(6, 8, cos_step, 0)
    next(ar_g)
    next(ar_m)
    lax.fori_loop(0, 8, cos_join, 0)
    c1 = []
    for d in (1, 2, 3):
        zz, yy = plus(z, d), plus(y, d)
        c1.append(send(crecv.at[:, zz, 0:128], c1a.at[d - 1], to_z(zz)))
        c1.append(send(crecv.at[yy, :, 128:256], c1b.at[d - 1], to_y(yy)))
    next(ar_g)
    next(ar_m)
    next(ar_m)
    mixed = m_fin[...]
    mixed_t = mixed.T
    normal = exact(mixed_t, mixed)

    def factor_first(a):
        up, lo = eliminate(a[:128, :128])
        off = exact(lo, a[:128, 128:])
        return up, lo, off, a[128:, 128:] - exact(off.T, off)

    def factor_second(up, lo, off, rest):
        up2, lo2 = eliminate(rest)
        corner = -exact(lo2, exact(off.T, lo))
        zero = jnp.zeros((128, 128), F32)
        left = jnp.concatenate([lo, corner], axis=0)
        right = jnp.concatenate([zero, lo2], axis=0)
        inv = jnp.concatenate([left, right], axis=1)
        top = jnp.concatenate([up, off], axis=1)
        bottom = jnp.concatenate([zero, up2], axis=1)
        return inv, jnp.concatenate([top, bottom], axis=0)

    next(ar_g)
    first = factor_first(normal)
    next(ar_g)
    for cp in c1:
        cp.wait_recv()
    for n in range(4):
        h2a[n] = (crecv[n, z, 0:128, :] + c1a[0, n]) + (c1a[1, n] + c1a[2, n])
        h2b[n] = (crecv[y, n, 128:256, :] + c1b[0, n]) + (c1b[1, n] + c1b[2, n])
    c2 = []
    for d in (1, 2, 3):
        zz, yy = plus(z, d), plus(y, d)
        c2.append(send(h2a.at[yy], c2a.at[d - 1], to_y(yy)))
        c2.append(send(h2b.at[zz], c2b.at[d - 1], to_z(zz)))
    inverse, unused = factor_second(*first)
    next(ar_g)
    for cp in c2:
        cp.wait_recv()
    cbase = al(core * 256, 256)
    cfin[pl.ds(cbase, 128), :] = (h2a[y] + c2a[0]) + (c2a[1] + c2a[2])
    cfin[pl.ds(al(cbase + 128, 128), 128), :] = (h2b[z] + c2b[0]) + (c2b[1] + c2b[2])
    cc = send(cfin.at[mine], cfin.at[mine], to_core())
    solve = exact(inverse.T, exact(inverse, mixed_t))
    cc.wait_recv()
    block = exact(solve, cfin[...])
    half = al(core * 128, 128)
    jbuf[...] = block
    ra = pl.ds(half, 64)
    rb = pl.ds(al(half + 64, 64), 64)
    xbuf[y, z, ra] = jbuf[ra, :]
    xbuf[y, z, rb] = jbuf[rb, :]
    x1 = []
    for d in (1, 2, 3):
        x1.append(send(xbuf.at[y, z, ra], xbuf.at[y, z, ra], to_z(plus(z, d))))
        x1.append(send(xbuf.at[y, z, rb], xbuf.at[y, z, rb], to_y(plus(y, d))))
    next(ar_g)
    next(ar_g)
    for cp in scopies:
        cp.wait_recv()
    gram = jnp.concatenate([g_fin[0:256, :], g_fin[256:512, :]], axis=1)
    for cp in x1:
        cp.wait_recv()
    x2, forward = [], []
    for d in (1, 2, 3):
        x2.append(send(xbuf.at[y, :, ra], xbuf.at[y, :, ra], to_y(plus(y, d))))
        x2.append(send(xbuf.at[:, z, rb], xbuf.at[:, z, rb], to_z(plus(z, d))))
    forward.append(send(xbuf.at[y, :, ra], xbuf.at[y, :, ra], to_core()))
    forward.append(send(xbuf.at[:, z, rb], xbuf.at[:, z, rb], to_core()))
    first = factor_first(gram)
    for d, (ca, cb) in zip((1, 2, 3), zip(x2[0::2], x2[1::2])):
        ca.wait_recv()
        cb.wait_recv()
        yy, zz = plus(y, 4 - d), plus(z, 4 - d)
        forward.append(send(xbuf.at[yy, :, ra], xbuf.at[yy, :, ra], to_core()))
        forward.append(send(xbuf.at[:, zz, rb], xbuf.at[:, zz, rb], to_core()))
    inverse, upper = factor_second(*first)
    j_out[...] = inverse
    r_out[...] = upper
    for cp in forward:
        cp.wait_recv()
    for cp in sent:
        cp.wait_send()

    def drain(j, carry):
        core_copy(j).wait_send()
        return carry

    lax.fori_loop(0, 8, drain, 0)


def last(scale, field, s, xb, inv, up, left, right, residual, sh, sl):
    @pl.when(pl.program_id(0) == 0)
    def _():
        high, low = halves(s[...])
        sh[...] = high
        sl[...] = low

    j = pl.program_id(0)
    cols = pl.ds(pl.multiple_of(j * 256, 256), 256)
    row, first = j // 2, lax.rem(j, 2) * 2
    block = jnp.concatenate([xb[row, first], xb[row, first + 1]], axis=1)
    xh, xl = halves(block)
    residual[...] = field[:, cols] - mm3(sh[...], sl[...], xh, xl)
    uh, ul = halves(up[...])
    right[...] = mm3(uh, ul, xh, xl)
    ih, il = halves(inv[...].T)
    rows = pl.ds(pl.multiple_of(j * 128, 128), 128)
    left[...] = mm3(sh[rows, :], sl[rows, :], ih, il) * scale


def per_device(cells, field, range_test, corange_test):
    def vm(*shape, dtype=F32):
        return pltpu.VMEM(shape, dtype)

    def reduce_buffers(w):
        return [
            vm(512, w), vm(256, w), vm(256, w), vm(2, 3, 32, w), vm(2, 32, w),
            vm(2, 3, 8, w), vm(4, 16, w), vm(512, w),
        ]

    any_space = pl.BlockSpec(memory_space=pl.ANY)
    here = pl.BlockSpec(memory_space=pltpu.VMEM)
    copy, s, xb, inv, up = pl.pallas_call(
        kernel,
        out_shape=(vm(1024, 2048), vm(1024, 256), vm(4, 4, 256, 128), vm(256, 256), vm(256, 256)),
        in_specs=[any_space] * 3,
        out_specs=[here] * 5,
        scratch_shapes=[
            vm(2048, 256), vm(512, 1024),
            vm(1024, 2048, dtype=BF16), vm(1024, 2048, dtype=BF16),
            vm(2048, 256, dtype=BF16), vm(2048, 256, dtype=BF16),
            vm(512, 1024, dtype=BF16), vm(512, 1024, dtype=BF16),
            vm(1024, 256), vm(3, 256, 256),
            vm(4, 4, 512, 128), vm(4, 4, 256, 128),
            vm(3, 4, 128, 128), vm(3, 4, 128, 128), vm(4, 128, 128), vm(4, 128, 128),
            vm(3, 128, 128), vm(3, 128, 128), vm(512, 128),
            *reduce_buffers(256),
            *reduce_buffers(128),
            vm(256, 128),
            pltpu.SemaphoreType.DMA((6,)),
            pltpu.SemaphoreType.DMA((120,)),
            pltpu.SemaphoreType.DMA((120,)),
            pltpu.SemaphoreType.DMA((8,)),
            pltpu.SemaphoreType.DMA((8,)),
        ],
        compiler_params=pltpu.CompilerParams(
            collective_id=0, has_side_effects=True, vmem_limit_bytes=44 * 1024 * 1024),
        name="sketch",
    )(field, range_test, corange_test)
    return pl.pallas_call(
        functools.partial(last, float(cells) ** 0.5),
        grid=(8,),
        out_shape=(
            jax.ShapeDtypeStruct((1024, 256), F32),
            jax.ShapeDtypeStruct((256, 2048), F32),
            jax.ShapeDtypeStruct((1024, 2048), F32),
        ),
        in_specs=[here] * 5,
        out_specs=(
            pl.BlockSpec((128, 256), lambda j: (j, 0)),
            pl.BlockSpec((256, 256), lambda j: (0, j)),
            pl.BlockSpec((1024, 256), lambda j: (0, j)),
        ),
        scratch_shapes=[vm(1024, 256, dtype=BF16), vm(1024, 256, dtype=BF16)],
        compiler_params=pltpu.CompilerParams(vmem_limit_bytes=32 * 1024 * 1024),
        name="finish",
    )(copy, s, xb, inv, up)


def solution(mesh):
    cells = 1024 * mesh.shape["space"]
    return jax.shard_map(
        functools.partial(per_device, cells),
        mesh=mesh,
        in_specs=(P("space", "tm"), P("tm", None), P(None, "space")),
        out_specs=(P("space", None), P(None, "tm"), P("space", "tm")),
        check_vma=False,
    )
```

```python
import functools

import jax
import jax.numpy as jnp
from jax import lax
from jax.experimental import pallas as pl
from jax.experimental.pallas import tpu as pltpu
from jax.sharding import PartitionSpec as P

MESH = pl.DeviceIdType.MESH
F32, BF16 = jnp.float32, jnp.bfloat16
HI = lax.Precision.HIGHEST


def halves(x):
    high = x.astype(BF16)
    return high, (x - high.astype(F32)).astype(BF16)


def mm(a, b):
    return jnp.dot(a, b, preferred_element_type=F32)


def mm3(ah, al, bh, bl):
    return mm(ah, bh) + (mm(ah, bl) + mm(al, bh))


def exact(a, b):
    return jnp.dot(a, b, preferred_element_type=F32, precision=HI)


def eliminate(matrix, between):
    lane = lax.broadcasted_iota(jnp.int32, (8, 128), 1)
    sub = lax.broadcasted_iota(jnp.int32, (8, 128), 0)

    def spread(v, index):
        return jnp.take_along_axis(v, index, axis=1, mode="promise_in_bounds")

    def level(v, i):
        return jnp.broadcast_to(v[i : i + 1, :], (8, 128))

    def tree(terms):
        while len(terms) > 1:
            terms = [terms[k] + terms[k + 1] for k in range(0, len(terms), 2)]
        return terms[0]

    def group(active, g, carry):
        before, *blocks = carry
        index = [jnp.full((8, 128), 8 * g + i, jnp.int32) for i in range(8)]
        past = [jnp.maximum(v - 8, 0) for v in index]
        inside_past = (lane >= 8 * g - 8) & (lane < 8 * g)
        inside = (lane >= 8 * g) & (lane < 8 * g + 8)
        w = kept = blocks[0]
        cols = [spread(w, k) for k in index]
        old_rows = [level(before, i) for i in range(8)]
        out = {b: jnp.where(inside_past, 0.0, blocks[b]) for b in range(1, active + 1)}
        first = [spread(blocks[1], past[i]) * old_rows[i] for i in range(8)]
        out[1] = out[1] - tree(first)
        ahead = [spread(out[1], k) for k in index]
        for i in range(8):
            at = lane == index[i]
            inv = 1.0 / level(cols[i], i)
            row = jnp.where(at, 1.0, level(w, i))
            mine = sub == i
            kept = jnp.where(mine, w, kept)
            w = jnp.where(mine, row * inv, jnp.where(at, 0.0, w) - (cols[i] * row) * inv)
            for m in range(i + 1, 8):
                r = level(cols[m], i)
                cols[m] = jnp.where(mine, r * inv, cols[m] - (cols[i] * r) * inv)
            for b in range(2, active + 1):
                out[b] = out[b] - spread(blocks[b], past[i]) * old_rows[i]
        new = list(blocks)
        for b in range(2, active + 1):
            new[b] = jnp.where(b < 16 - g, out[b], blocks[b])
        pivot = jnp.where(inside, 0.0, out[1]) - tree([ahead[i] * level(w, i) for i in range(8)])
        new[1] = jnp.where(g < 15, pivot, blocks[1])
        return (w, *new[1:], kept)

    carry = (jnp.zeros((8, 128), F32), *(matrix[8 * b : 8 * b + 8, :] for b in range(16)))
    for n, active in enumerate((15, 11, 7, 3)):
        carry = lax.fori_loop(4 * n, 4 * n + 4, functools.partial(group, active), carry)
        between()
    full = jnp.concatenate(carry[1:], axis=0)
    r = lax.broadcasted_iota(jnp.int32, (128, 128), 0)
    c = lax.broadcasted_iota(jnp.int32, (128, 128), 1)
    diag = jnp.sum(jnp.where(r == c, full, 0.0), axis=1, keepdims=True)
    scale = 1.0 / jnp.sqrt(diag)
    upper = jnp.where(c >= r, full, 0.0) * scale
    lower = jnp.where(c < r, full, jnp.where(c == r, 1.0, 0.0)) * scale
    return upper, lower


def kernel(
    field, rng, cor, fbuf, sbuf, xbuf, j_out, r_out,
    rbuf, obuf, fh, fl, rh, rl, oh, ol,
    part, precv,
    cpart, crecv, c1, s1, t1, o1, u2, s2, w2, cfin,
    m_part, m_r0, m_h1, m_r1, m_h2, m_r2, m_r3, m_fin,
    g_part, g_r1, g_h2, g_r2, g_sw, g_swr, g_r3, g_fin,
    jbuf,
    lsem, ssem, rsem, csend, crecvs,
):
    x = lax.axis_index("tm")
    sp = lax.axis_index("space")
    core = lax.rem(sp, 2)
    z = lax.rem(sp // 2, 4)
    y = sp // 8
    oc = 1 - core

    def plus(v, d):
        return lax.rem(v + d, 4)

    def flip(v, e):
        return (v, v + 1 - 2 * lax.rem(v, 2), plus(v, 2), 3 - v)[e]

    def to_core():
        return {"space": sp + 1 - 2 * core}

    def to_z(zz):
        return {"space": y * 8 + zz * 2 + core}

    def to_y(yy):
        return {"space": yy * 8 + z * 2 + core}

    def to_x(xx):
        return {"tm": xx}

    def al(v, n):
        return pl.multiple_of(v, n)

    count = [0]
    sent = []

    def send(src, dst, peer):
        i = count[0]
        count[0] += 1
        copy = pltpu.make_async_remote_copy(
            src_ref=src, dst_ref=dst, send_sem=ssem.at[i], recv_sem=rsem.at[i],
            device_id=peer, device_id_type=MESH)
        copy.start()
        sent.append(copy)
        return copy

    loads = [pltpu.make_async_copy(rng, rbuf, lsem.at[0])]
    order = (2, 1, 3, 0)
    for n, d in enumerate(order):
        rows = pl.ds(al(plus(x, d) * 256, 256), 256)
        loads.append(pltpu.make_async_copy(field.at[rows], fbuf.at[rows], lsem.at[1 + n]))
    loads.append(pltpu.make_async_copy(cor, obuf, lsem.at[5]))
    for load in loads:
        load.start()

    barrier = pltpu.get_barrier_semaphore()
    peers = [to_core()]
    for d in (1, 2, 3):
        peers += [to_z(plus(z, d)), to_y(plus(y, d)), to_x(plus(x, d))]
    for peer in peers:
        pl.semaphore_signal(barrier, inc=1, device_id=peer, device_id_type=MESH)

    def all_reduce(w, part, r0, h1, r1, h2, r2, r3, fin):
        base = al(core * 256, 256)
        cp = send(part.at[pl.ds(al(oc * 256, 256), 256)], r0, to_core())
        yield
        cp.wait_recv()
        h1[...] = part[pl.ds(base, 256), :] + r0[...]
        cps = []
        for d in (1, 2, 3):
            zz, yy = plus(z, d), plus(y, d)
            cps.append(send(h1.at[pl.ds(al(32 * zz, 32), 32)], r1.at[0, d - 1], to_z(zz)))
            cps.append(send(h1.at[pl.ds(al(128 + 32 * yy, 32), 32)], r1.at[1, d - 1], to_y(yy)))
        yield
        for cp in cps:
            cp.wait_recv()
        for k, v in ((0, z), (1, y)):
            h2[k] = (h1[pl.ds(al(128 * k + 32 * v, 32), 32), :] + r1[k, 0]) + (r1[k, 1] + r1[k, 2])
        cps = []
        for d in (1, 2, 3):
            zz, yy = plus(z, d), plus(y, d)
            cps.append(send(h2.at[0, pl.ds(al(8 * yy, 8), 8)], r2.at[0, d - 1], to_y(yy)))
            cps.append(send(h2.at[1, pl.ds(al(8 * zz, 8), 8)], r2.at[1, d - 1], to_z(zz)))
        yield
        for cp in cps:
            cp.wait_recv()
        for k, v in ((0, y), (1, z)):
            r3[x, 8 * k : 8 * k + 8, :] = (h2[k, pl.ds(al(8 * v, 8), 8), :] + r2[k, 0]) + (r2[k, 1] + r2[k, 2])
        cps = [send(r3.at[x], r3.at[x], to_x(plus(x, d))) for d in (1, 2, 3)]
        yield
        for cp in cps:
            cp.wait_recv()
        total = (r3[0] + r3[1]) + (r3[2] + r3[3])
        a = al(base + 32 * z, 32)
        b = al(base + 128 + 32 * y, 32)
        a8 = pl.ds(al(a + 8 * y, 8), 8)
        b8 = pl.ds(al(b + 8 * z, 8), 8)
        fin[a8, :] = total[0:8]
        fin[b8, :] = total[8:16]
        cps = []
        for d in (1, 2, 3):
            cps.append(send(fin.at[a8], fin.at[a8], to_y(plus(y, d))))
            cps.append(send(fin.at[b8], fin.at[b8], to_z(plus(z, d))))
        yield
        for cp in cps:
            cp.wait_recv()
        a32, b32 = pl.ds(a, 32), pl.ds(b, 32)
        cps = []
        for d in (1, 2, 3):
            cps.append(send(fin.at[a32], fin.at[a32], to_z(plus(z, d))))
            cps.append(send(fin.at[b32], fin.at[b32], to_y(plus(y, d))))
        yield
        for cp in cps:
            cp.wait_recv()
        mine = pl.ds(base, 256)
        cp = send(fin.at[mine], fin.at[mine], to_core())
        yield
        cp.wait_recv()
        yield

    def all_reduce_late(part, r1, h2, r2, sw, swr, r3, fin):
        cps = []
        for d in (1, 2, 3):
            zz, yy = plus(z, d), plus(y, d)
            cps.append(send(part.at[pl.ds(al(64 * zz, 64), 64)], r1.at[0, d - 1], to_z(zz)))
            cps.append(send(part.at[pl.ds(al(256 + 64 * yy, 64), 64)], r1.at[1, d - 1], to_y(yy)))
        yield
        for cp in cps:
            cp.wait_recv()
        for k, v in ((0, z), (1, y)):
            h2[k] = (part[pl.ds(al(256 * k + 64 * v, 64), 64), :] + r1[k, 0]) + (r1[k, 1] + r1[k, 2])
        cps = []
        for d in (1, 2, 3):
            zz, yy = plus(z, d), plus(y, d)
            cps.append(send(h2.at[0, pl.ds(al(16 * yy, 16), 16)], r2.at[0, d - 1], to_y(yy)))
            cps.append(send(h2.at[1, pl.ds(al(16 * zz, 16), 16)], r2.at[1, d - 1], to_z(zz)))
        yield
        for cp in cps:
            cp.wait_recv()
        for k, v in ((0, y), (1, z)):
            sw[16 * k : 16 * k + 16, :] = (h2[k, pl.ds(al(16 * v, 16), 16), :] + r2[k, 0]) + (r2[k, 1] + r2[k, 2])
        cp = send(sw, swr, to_core())
        yield
        cp.wait_recv()
        r3[x] = sw[...] + swr[...]
        cps = [send(r3.at[x], r3.at[x], to_x(plus(x, d))) for d in (1, 2, 3)]
        yield
        for cp in cps:
            cp.wait_recv()
        total = (r3[0] + r3[1]) + (r3[2] + r3[3])
        a = al(64 * z, 64)
        b = al(256 + 64 * y, 64)
        a16 = pl.ds(al(a + 16 * y, 16), 16)
        b16 = pl.ds(al(b + 16 * z, 16), 16)
        fin[a16, :] = total[0:16]
        fin[b16, :] = total[16:32]
        cps = []
        for d in (1, 2, 3):
            cps.append(send(fin.at[a16], fin.at[a16], to_y(plus(y, d))))
            cps.append(send(fin.at[b16], fin.at[b16], to_z(plus(z, d))))
        yield
        for cp in cps:
            cp.wait_recv()
        a64, b64 = pl.ds(a, 64), pl.ds(b, 64)
        cps = []
        for d in (1, 2, 3):
            cps.append(send(fin.at[a64], fin.at[a64], to_z(plus(z, d))))
            cps.append(send(fin.at[b64], fin.at[b64], to_y(plus(y, d))))
        yield
        for cp in cps:
            cp.wait_recv()
        yield

    loads[0].wait()
    high, low = halves(rbuf[...])
    rh[...] = high
    rl[...] = low
    pcopies = []
    for n, d in enumerate(order):
        loads[1 + n].wait()
        xx = plus(x, d)
        rows = pl.ds(al(xx * 256, 256), 256)
        high, low = halves(fbuf[rows, :])
        fh[rows, :] = high
        fl[rows, :] = low
        part[rows, :] = mm3(fh[rows, :], fl[rows, :], rh[...], rl[...])
        if n == 0:
            pl.semaphore_wait(barrier, len(peers))
        if d:
            pcopies.append(send(part.at[rows], precv.at[d - 1], to_x(xx)))

    loads[5].wait()
    high, low = halves(obuf[...])
    oh[...] = high
    ol[...] = low
    high, low = halves(part[...])
    m_part[...] = mm3(oh[...], ol[...], high, low)
    ar_m = all_reduce(256, m_part, m_r0, m_h1, m_r1, m_h2, m_r2, m_r3, m_fin)
    next(ar_m)

    other = pl.ds(al(oc * 256, 256), 256)
    mine = pl.ds(al(core * 256, 256), 256)

    def core_copy(j):
        return pltpu.make_async_remote_copy(
            src_ref=cpart.at[j, :, other], dst_ref=crecv.at[j],
            send_sem=csend.at[j], recv_sem=crecvs.at[j], device_id=to_core(), device_id_type=MESH)

    def cos_step(j, carry):
        k = j // 2
        yy = jnp.where(k == 0, flip(y, 2), jnp.where(k == 1, flip(y, 1), jnp.where(k == 2, flip(y, 3), y)))
        even = lax.rem(j, 2) == 0
        za = jnp.where(even, flip(z, 2), flip(z, 3))
        zb = jnp.where(even, flip(z, 1), z)
        ca = pl.ds(al((yy * 4 + za) * 128, 128), 128)
        cb = pl.ds(al((yy * 4 + zb) * 128, 128), 128)
        bh = jnp.concatenate([fh[:, ca], fh[:, cb]], axis=1)
        bl = jnp.concatenate([fl[:, ca], fl[:, cb]], axis=1)
        block = mm3(oh[...], ol[...], bh, bl)
        cpart[j, 0] = block[:, :128]
        cpart[j, 1] = block[:, 128:]
        core_copy(j).start()
        return carry

    where = {}
    for j in range(8):
        for t, ez in enumerate((2, 1) if j % 2 == 0 else (3, 0)):
            where[(2, 1, 3, 0)[j // 2], ez] = (j, t)

    turns = ((1, 3), (3, 1))

    def over(p, stage):
        return (lambda e: to_z(flip(z, e))) if (p < 2) == (stage == 1) else (lambda e: to_y(flip(y, e)))

    def block_of(p, along, across):
        j, t = where[(across, along) if p < 2 else (along, across)]
        return crecv[j, t, 64 * p : 64 * p + 64, :]

    c_in = []

    def cos_join(j):
        core_copy(j).wait_recv()
        crecv[j] = crecv[j] + cpart[j, :, mine]
        for (ey, ez), (jj, t) in where.items():
            if jj != j:
                continue
            for p in range(4):
                along, across = (ez, ey) if p < 2 else (ey, ez)
                near = turns[p % 2][0]
                if along in (near, 2):
                    c_in.append(send(
                        crecv.at[j, t, 64 * p : 64 * p + 64], c1.at[p, int(along == 2), across], over(p, 1)(near)))

    def take(copies):
        for cp in copies:
            cp.wait_recv()
        del copies[:]

    def c_1b():
        take(c_in)
        for p in range(4):
            far = turns[p % 2][1]
            for n in range(4):
                s1[p, n] = block_of(p, far, n) + c1[p, 1, n]
            c_in.append(send(s1.at[p], t1.at[p], over(p, 1)(far)))

    def c_2a():
        take(c_in)
        for p in range(4):
            for n in range(4):
                o1[p, n] = (block_of(p, 0, n) + c1[p, 0, n]) + t1[p, n]
            near = turns[p % 2][0]
            lo = 1 if near == 1 else 2
            c_in.append(send(o1.at[p, lo : lo + 2], u2.at[p], over(p, 2)(near)))

    def c_2b():
        take(c_in)
        for p in range(4):
            near, far = turns[p % 2]
            s2[p] = o1[p, far] + u2[p, 1 if near == 1 else 0]
            c_in.append(send(s2.at[p], w2.at[p], over(p, 2)(far)))

    def c_end():
        take(c_in)
        for p in range(4):
            near = turns[p % 2][0]
            rows = pl.ds(al(core * 256 + 64 * p, 64), 64)
            cfin[rows, :] = (o1[p, 0] + u2[p, 0 if near == 1 else 1]) + w2[p]
        return send(cfin.at[mine], cfin.at[mine], to_core())

    lax.fori_loop(0, 2, cos_step, 0)
    next(ar_m)
    lax.fori_loop(2, 6, cos_step, 0)
    next(ar_m)
    cos_join(0)
    cos_join(1)
    lax.fori_loop(6, 8, cos_step, 0)
    next(ar_m)
    for cp in pcopies:
        cp.wait_recv()
    own = pl.ds(al(x * 256, 256), 256)
    rows_sum = (part[own, :] + precv[0]) + (precv[1] + precv[2])
    sbuf[own, :] = rows_sum
    gram = exact(rows_sum.T, rows_sum)
    g_part[0:256, :] = gram[:, :128]
    g_part[256:512, :] = gram[:, 128:]
    ar_g = all_reduce_late(g_part, g_r1, g_h2, g_r2, g_sw, g_swr, g_r3, g_fin)
    cos_join(2)
    cos_join(3)
    next(ar_m)
    next(ar_g)
    cos_join(4)
    cos_join(5)
    next(ar_m)
    scopies = [send(sbuf.at[own], sbuf.at[own], to_x(plus(x, d))) for d in (1, 2, 3)]
    cos_join(6)
    cos_join(7)
    next(ar_m)
    next(ar_g)
    next(ar_m)
    mixed = m_fin[...]
    mixed_t = mixed.T
    normal = exact(mixed_t, mixed)

    def factor_first(a, between):
        up, lo = eliminate(a[:128, :128], between)
        off = exact(lo, a[:128, 128:])
        return up, lo, off, a[128:, 128:] - exact(off.T, off)

    def factor_second(up, lo, off, rest, between):
        up2, lo2 = eliminate(rest, between)
        corner = -exact(lo2, exact(off.T, lo))
        zero = jnp.zeros((128, 128), F32)
        left = jnp.concatenate([lo, corner], axis=0)
        right = jnp.concatenate([zero, lo2], axis=0)
        inv = jnp.concatenate([left, right], axis=1)
        top = jnp.concatenate([up, off], axis=1)
        bottom = jnp.concatenate([zero, up2], axis=1)
        return inv, jnp.concatenate([top, bottom], axis=0)

    def queue(*steps):
        steps = list(steps)

        def run():
            if steps:
                steps.pop(0)()

        return run

    def step_g():
        next(ar_g)

    def rest():
        pass

    c_1b()
    first = factor_first(normal, queue(rest, step_g, step_g, c_2a))
    inverse, unused = factor_second(*first, queue(step_g, rest, c_2b, step_g))
    solve = exact(inverse.T, exact(inverse, mixed_t))
    cc = c_end()
    cc.wait_recv()
    block = exact(solve, cfin[...])
    half = al(core * 128, 128)
    jbuf[...] = block
    ra = pl.ds(half, 64)
    rb = pl.ds(al(half + 64, 64), 64)
    xbuf[y, z, ra] = jbuf[ra, :]
    xbuf[y, z, rb] = jbuf[rb, :]
    x1 = []
    for d in (1, 2, 3):
        x1.append(send(xbuf.at[y, z, ra], xbuf.at[y, z, ra], to_z(plus(z, d))))
        x1.append(send(xbuf.at[y, z, rb], xbuf.at[y, z, rb], to_y(plus(y, d))))
    next(ar_g)
    for cp in scopies:
        cp.wait_recv()
    gram = jnp.concatenate([g_fin[0:256, :], g_fin[256:512, :]], axis=1)

    forward = []

    def lot(p, e):
        rows = pl.ds(al(half + 32 * p, 32), 32)
        return xbuf.at[flip(y, e), :, rows] if p < 2 else xbuf.at[:, flip(z, e), rows]

    def x_2a():
        take(x1)
        for p in range(4):
            x1.append(send(lot(p, 0), lot(p, 0), over(p, 2)(turns[p % 2][1])))
        for p in range(4):
            forward.append(send(lot(p, 0), lot(p, 0), to_core()))

    x_last = []

    def x_2b():
        for p in range(4):
            near = turns[p % 2][0]
            x_last.append(send(lot(p, 0), lot(p, 0), over(p, 2)(near)))
        take(x1)
        for p in range(4):
            near, far = turns[p % 2]
            x_last.append(send(lot(p, far), lot(p, far), over(p, 2)(near)))
        for p in range(4):
            far = turns[p % 2][1]
            forward.append(send(lot(p, far), lot(p, far), to_core()))

    def x_end(part):
        for p in range(4):
            near, far = turns[p % 2]
            x_last[4 * part + p].wait_recv()
            e = near if part == 0 else 2
            forward.append(send(lot(p, e), lot(p, e), to_core()))

    first = factor_first(gram, queue(rest, rest, x_2a))
    inverse, upper = factor_second(*first, queue(x_2b, rest, rest, lambda: x_end(0)))
    x_end(1)
    j_out[...] = inverse
    r_out[...] = upper
    for cp in forward:
        cp.wait_recv()
    for cp in sent:
        cp.wait_send()

    def drain(j, carry):
        core_copy(j).wait_send()
        return carry

    lax.fori_loop(0, 8, drain, 0)


def last(scale, field, s, xb, inv, up, left, right, residual, sh, sl):
    @pl.when(pl.program_id(0) == 0)
    def _():
        high, low = halves(s[...])
        sh[...] = high
        sl[...] = low

    j = pl.program_id(0)
    cols = pl.ds(pl.multiple_of(j * 256, 256), 256)
    row, first = j // 2, lax.rem(j, 2) * 2
    block = jnp.concatenate([xb[row, first], xb[row, first + 1]], axis=1)
    xh, xl = halves(block)
    residual[...] = field[:, cols] - mm3(sh[...], sl[...], xh, xl)
    uh, ul = halves(up[...])
    right[...] = mm3(uh, ul, xh, xl)
    ih, il = halves(inv[...].T)
    rows = pl.ds(pl.multiple_of(j * 128, 128), 128)
    left[...] = mm3(sh[rows, :], sl[rows, :], ih, il) * scale


def per_device(cells, field, range_test, corange_test):
    def vm(*shape, dtype=F32):
        return pltpu.VMEM(shape, dtype)

    def reduce_buffers(w):
        return [
            vm(512, w), vm(256, w), vm(256, w), vm(2, 3, 32, w), vm(2, 32, w),
            vm(2, 3, 8, w), vm(4, 16, w), vm(512, w),
        ]

    any_space = pl.BlockSpec(memory_space=pl.ANY)
    here = pl.BlockSpec(memory_space=pltpu.VMEM)
    copy, s, xb, inv, up = pl.pallas_call(
        kernel,
        out_shape=(vm(1024, 2048), vm(1024, 256), vm(4, 4, 256, 128), vm(256, 256), vm(256, 256)),
        in_specs=[any_space] * 3,
        out_specs=[here] * 5,
        scratch_shapes=[
            vm(2048, 256), vm(512, 1024),
            vm(1024, 2048, dtype=BF16), vm(1024, 2048, dtype=BF16),
            vm(2048, 256, dtype=BF16), vm(2048, 256, dtype=BF16),
            vm(512, 1024, dtype=BF16), vm(512, 1024, dtype=BF16),
            vm(1024, 256), vm(3, 256, 256),
            vm(8, 2, 512, 128), vm(8, 2, 256, 128),
            vm(4, 2, 4, 64, 128), vm(4, 4, 64, 128), vm(4, 4, 64, 128), vm(4, 4, 64, 128),
            vm(4, 2, 64, 128), vm(4, 64, 128), vm(4, 64, 128), vm(512, 128),
            *reduce_buffers(256),
            vm(512, 128), vm(2, 3, 64, 128), vm(2, 64, 128), vm(2, 3, 16, 128),
            vm(32, 128), vm(32, 128), vm(4, 32, 128), vm(512, 128),
            vm(256, 128),
            pltpu.SemaphoreType.DMA((6,)),
            pltpu.SemaphoreType.DMA((180,)),
            pltpu.SemaphoreType.DMA((180,)),
            pltpu.SemaphoreType.DMA((8,)),
            pltpu.SemaphoreType.DMA((8,)),
        ],
        compiler_params=pltpu.CompilerParams(
            collective_id=0, has_side_effects=True, vmem_limit_bytes=44 * 1024 * 1024),
        name="sketch",
    )(field, range_test, corange_test)
    return pl.pallas_call(
        functools.partial(last, float(cells) ** 0.5),
        grid=(8,),
        out_shape=(
            jax.ShapeDtypeStruct((1024, 256), F32),
            jax.ShapeDtypeStruct((256, 2048), F32),
            jax.ShapeDtypeStruct((1024, 2048), F32),
        ),
        in_specs=[here] * 5,
        out_specs=(
            pl.BlockSpec((128, 256), lambda j: (j, 0)),
            pl.BlockSpec((256, 256), lambda j: (0, j)),
            pl.BlockSpec((1024, 256), lambda j: (0, j)),
        ),
        scratch_shapes=[vm(1024, 256, dtype=BF16), vm(1024, 256, dtype=BF16)],
        compiler_params=pltpu.CompilerParams(vmem_limit_bytes=32 * 1024 * 1024),
        name="finish",
    )(copy, s, xb, inv, up)


def solution(mesh):
    cells = 1024 * mesh.shape["space"]
    return jax.shard_map(
        functools.partial(per_device, cells),
        mesh=mesh,
        in_specs=(P("space", "tm"), P("tm", None), P(None, "space")),
        out_specs=(P("space", None), P(None, "tm"), P("space", "tm")),
        check_vma=False,
    )
```

```python
import functools

import jax
import jax.numpy as jnp
from jax import lax
from jax.experimental import pallas as pl
from jax.experimental.pallas import tpu as pltpu
from jax.sharding import PartitionSpec as P

MESH = pl.DeviceIdType.MESH
F32, BF16 = jnp.float32, jnp.bfloat16
HI = lax.Precision.HIGHEST


def halves(x):
    high = x.astype(BF16)
    return high, (x - high.astype(F32)).astype(BF16)


def mm(a, b):
    return jnp.dot(a, b, preferred_element_type=F32)


def mm3(ah, al, bh, bl):
    return mm(ah, bh) + (mm(ah, bl) + mm(al, bh))


def exact(a, b):
    return jnp.dot(a, b, preferred_element_type=F32, precision=HI)


def eliminate(matrix, between):
    lane = lax.broadcasted_iota(jnp.int32, (8, 128), 1)
    sub = lax.broadcasted_iota(jnp.int32, (8, 128), 0)

    def spread(v, index):
        return jnp.take_along_axis(v, index, axis=1, mode="promise_in_bounds")

    def level(v, i):
        return jnp.broadcast_to(v[i : i + 1, :], (8, 128))

    def tree(terms):
        while len(terms) > 1:
            terms = [terms[k] + terms[k + 1] for k in range(0, len(terms), 2)]
        return terms[0]

    def group(active, g, carry):
        before, *blocks = carry
        index = [jnp.full((8, 128), 8 * g + i, jnp.int32) for i in range(8)]
        past = [jnp.maximum(v - 8, 0) for v in index]
        inside_past = (lane >= 8 * g - 8) & (lane < 8 * g)
        inside = (lane >= 8 * g) & (lane < 8 * g + 8)
        w = kept = blocks[0]
        cols = [spread(w, k) for k in index]
        old_rows = [level(before, i) for i in range(8)]
        out = {b: jnp.where(inside_past, 0.0, blocks[b]) for b in range(1, active + 1)}
        first = [spread(blocks[1], past[i]) * old_rows[i] for i in range(8)]
        out[1] = out[1] - tree(first)
        ahead = [spread(out[1], k) for k in index]
        for i in range(8):
            at = lane == index[i]
            inv = 1.0 / level(cols[i], i)
            row = jnp.where(at, 1.0, level(w, i))
            mine = sub == i
            kept = jnp.where(mine, w, kept)
            w = jnp.where(mine, row * inv, jnp.where(at, 0.0, w) - (cols[i] * row) * inv)
            for m in range(i + 1, 8):
                r = level(cols[m], i)
                cols[m] = jnp.where(mine, r * inv, cols[m] - (cols[i] * r) * inv)
            for b in range(2, active + 1):
                out[b] = out[b] - spread(blocks[b], past[i]) * old_rows[i]
        new = list(blocks)
        for b in range(2, active + 1):
            new[b] = jnp.where(b < 16 - g, out[b], blocks[b])
        pivot = jnp.where(inside, 0.0, out[1]) - tree([ahead[i] * level(w, i) for i in range(8)])
        new[1] = jnp.where(g < 15, pivot, blocks[1])
        return (w, *new[1:], kept)

    carry = (jnp.zeros((8, 128), F32), *(matrix[8 * b : 8 * b + 8, :] for b in range(16)))
    for n, active in enumerate((15, 11, 7, 3)):
        carry = lax.fori_loop(4 * n, 4 * n + 4, functools.partial(group, active), carry)
        between()
    full = jnp.concatenate(carry[1:], axis=0)
    r = lax.broadcasted_iota(jnp.int32, (128, 128), 0)
    c = lax.broadcasted_iota(jnp.int32, (128, 128), 1)
    diag = jnp.sum(jnp.where(r == c, full, 0.0), axis=1, keepdims=True)
    scale = 1.0 / jnp.sqrt(diag)
    upper = jnp.where(c >= r, full, 0.0) * scale
    lower = jnp.where(c < r, full, jnp.where(c == r, 1.0, 0.0)) * scale
    return upper, lower


def kernel(
    field, rng, cor, fbuf, sbuf, xbuf, j_out, r_out,
    rbuf, obuf, fh, fl, rh, rl, oh, ol,
    part, precv,
    cpart, crecv, c1, s1, t1, o1, u2, s2, w2, cfin,
    m_part, m_r0, m_h1, m_r1, m_h2, m_r2, m_r3, m_fin,
    g_part, g_r1, g_h2, g_r2, g_sw, g_swr, g_r3, g_fin,
    jbuf,
    lsem, ssem, rsem, csend, crecvs,
):
    x = lax.axis_index("tm")
    sp = lax.axis_index("space")
    core = lax.rem(sp, 2)
    z = lax.rem(sp // 2, 4)
    y = sp // 8
    oc = 1 - core

    def plus(v, d):
        return lax.rem(v + d, 4)

    def flip(v, e):
        return (v, v + 1 - 2 * lax.rem(v, 2), plus(v, 2), 3 - v)[e]

    def to_core():
        return {"space": sp + 1 - 2 * core}

    def to_z(zz):
        return {"space": y * 8 + zz * 2 + core}

    def to_y(yy):
        return {"space": yy * 8 + z * 2 + core}

    def to_x(xx):
        return {"tm": xx}

    def al(v, n):
        return pl.multiple_of(v, n)

    count = [0]
    sent = []

    def send(src, dst, peer):
        i = count[0]
        count[0] += 1
        copy = pltpu.make_async_remote_copy(
            src_ref=src, dst_ref=dst, send_sem=ssem.at[i], recv_sem=rsem.at[i],
            device_id=peer, device_id_type=MESH)
        copy.start()
        sent.append(copy)
        return copy

    loads = [pltpu.make_async_copy(rng, rbuf, lsem.at[0])]
    order = (2, 1, 3, 0)
    for n, d in enumerate(order):
        rows = pl.ds(al(plus(x, d) * 256, 256), 256)
        loads.append(pltpu.make_async_copy(field.at[rows], fbuf.at[rows], lsem.at[1 + n]))
    loads.append(pltpu.make_async_copy(cor, obuf, lsem.at[5]))
    for load in loads:
        load.start()

    barrier = pltpu.get_barrier_semaphore()
    peers = [to_core()]
    for d in (1, 2, 3):
        peers += [to_z(plus(z, d)), to_y(plus(y, d)), to_x(plus(x, d))]
    for peer in peers:
        pl.semaphore_signal(barrier, inc=1, device_id=peer, device_id_type=MESH)

    def all_reduce(w, part, r0, h1, r1, h2, r2, r3, fin):
        base = al(core * 256, 256)
        cp = send(part.at[pl.ds(al(oc * 256, 256), 256)], r0, to_core())
        yield
        cp.wait_recv()
        h1[...] = part[pl.ds(base, 256), :] + r0[...]
        cps = []
        for d in (1, 2, 3):
            zz, yy = plus(z, d), plus(y, d)
            cps.append(send(h1.at[pl.ds(al(32 * zz, 32), 32)], r1.at[0, d - 1], to_z(zz)))
            cps.append(send(h1.at[pl.ds(al(128 + 32 * yy, 32), 32)], r1.at[1, d - 1], to_y(yy)))
        yield
        for cp in cps:
            cp.wait_recv()
        for k, v in ((0, z), (1, y)):
            h2[k] = (h1[pl.ds(al(128 * k + 32 * v, 32), 32), :] + r1[k, 0]) + (r1[k, 1] + r1[k, 2])
        cps = []
        for d in (1, 2, 3):
            zz, yy = plus(z, d), plus(y, d)
            cps.append(send(h2.at[0, pl.ds(al(8 * yy, 8), 8)], r2.at[0, d - 1], to_y(yy)))
            cps.append(send(h2.at[1, pl.ds(al(8 * zz, 8), 8)], r2.at[1, d - 1], to_z(zz)))
        yield
        for cp in cps:
            cp.wait_recv()
        for k, v in ((0, y), (1, z)):
            r3[x, 8 * k : 8 * k + 8, :] = (h2[k, pl.ds(al(8 * v, 8), 8), :] + r2[k, 0]) + (r2[k, 1] + r2[k, 2])
        cps = [send(r3.at[x], r3.at[x], to_x(plus(x, d))) for d in (1, 2, 3)]
        yield
        for cp in cps:
            cp.wait_recv()
        total = (r3[0] + r3[1]) + (r3[2] + r3[3])
        a = al(base + 32 * z, 32)
        b = al(base + 128 + 32 * y, 32)
        a8 = pl.ds(al(a + 8 * y, 8), 8)
        b8 = pl.ds(al(b + 8 * z, 8), 8)
        fin[a8, :] = total[0:8]
        fin[b8, :] = total[8:16]
        cps = []
        for d in (1, 2, 3):
            cps.append(send(fin.at[a8], fin.at[a8], to_y(plus(y, d))))
            cps.append(send(fin.at[b8], fin.at[b8], to_z(plus(z, d))))
        yield
        for cp in cps:
            cp.wait_recv()
        a32, b32 = pl.ds(a, 32), pl.ds(b, 32)
        cps = []
        for d in (1, 2, 3):
            cps.append(send(fin.at[a32], fin.at[a32], to_z(plus(z, d))))
            cps.append(send(fin.at[b32], fin.at[b32], to_y(plus(y, d))))
        yield
        for cp in cps:
            cp.wait_recv()
        mine = pl.ds(base, 256)
        cp = send(fin.at[mine], fin.at[mine], to_core())
        yield
        cp.wait_recv()
        yield

    def all_reduce_late(part, r1, h2, r2, sw, swr, r3, fin):
        cps = []
        for d in (1, 2, 3):
            zz, yy = plus(z, d), plus(y, d)
            cps.append(send(part.at[pl.ds(al(64 * zz, 64), 64)], r1.at[0, d - 1], to_z(zz)))
            cps.append(send(part.at[pl.ds(al(256 + 64 * yy, 64), 64)], r1.at[1, d - 1], to_y(yy)))
        yield
        for cp in cps:
            cp.wait_recv()
        for k, v in ((0, z), (1, y)):
            h2[k] = (part[pl.ds(al(256 * k + 64 * v, 64), 64), :] + r1[k, 0]) + (r1[k, 1] + r1[k, 2])
        cps = []
        for d in (1, 2, 3):
            zz, yy = plus(z, d), plus(y, d)
            cps.append(send(h2.at[0, pl.ds(al(16 * yy, 16), 16)], r2.at[0, d - 1], to_y(yy)))
            cps.append(send(h2.at[1, pl.ds(al(16 * zz, 16), 16)], r2.at[1, d - 1], to_z(zz)))
        yield
        for cp in cps:
            cp.wait_recv()
        for k, v in ((0, y), (1, z)):
            sw[16 * k : 16 * k + 16, :] = (h2[k, pl.ds(al(16 * v, 16), 16), :] + r2[k, 0]) + (r2[k, 1] + r2[k, 2])
        cp = send(sw, swr, to_core())
        yield
        cp.wait_recv()
        r3[x] = sw[...] + swr[...]
        cps = [send(r3.at[x], r3.at[x], to_x(plus(x, d))) for d in (1, 2, 3)]
        yield
        for cp in cps:
            cp.wait_recv()
        total = (r3[0] + r3[1]) + (r3[2] + r3[3])
        a = al(64 * z, 64)
        b = al(256 + 64 * y, 64)
        a16 = pl.ds(al(a + 16 * y, 16), 16)
        b16 = pl.ds(al(b + 16 * z, 16), 16)
        fin[a16, :] = total[0:16]
        fin[b16, :] = total[16:32]
        cps = []
        for d in (1, 2, 3):
            cps.append(send(fin.at[a16], fin.at[a16], to_y(plus(y, d))))
            cps.append(send(fin.at[b16], fin.at[b16], to_z(plus(z, d))))
        yield
        for cp in cps:
            cp.wait_recv()
        a64, b64 = pl.ds(a, 64), pl.ds(b, 64)
        cps = []
        for d in (1, 2, 3):
            cps.append(send(fin.at[a64], fin.at[a64], to_z(plus(z, d))))
            cps.append(send(fin.at[b64], fin.at[b64], to_y(plus(y, d))))
        yield
        for cp in cps:
            cp.wait_recv()
        yield

    loads[0].wait()
    high, low = halves(rbuf[...])
    rh[...] = high
    rl[...] = low
    pcopies = []
    for n, d in enumerate(order):
        loads[1 + n].wait()
        xx = plus(x, d)
        rows = pl.ds(al(xx * 256, 256), 256)
        high, low = halves(fbuf[rows, :])
        fh[rows, :] = high
        fl[rows, :] = low
        part[rows, :] = mm3(high, low, rh[...], rl[...])
        if n == 0:
            pl.semaphore_wait(barrier, len(peers))
        if d:
            pcopies.append(send(part.at[rows], precv.at[d - 1], to_x(xx)))

    loads[5].wait()
    high, low = halves(obuf[...])
    oh[...] = high
    ol[...] = low
    high, low = halves(part[...])
    m_part[...] = mm3(oh[...], ol[...], high, low)
    ar_m = all_reduce(256, m_part, m_r0, m_h1, m_r1, m_h2, m_r2, m_r3, m_fin)
    next(ar_m)

    other = pl.ds(al(oc * 256, 256), 256)
    mine = pl.ds(al(core * 256, 256), 256)

    def core_copy(j):
        return pltpu.make_async_remote_copy(
            src_ref=cpart.at[j, :, other], dst_ref=crecv.at[j],
            send_sem=csend.at[j], recv_sem=crecvs.at[j], device_id=to_core(), device_id_type=MESH)

    def cos_step(j, carry):
        k = j // 2
        yy = jnp.where(k == 0, flip(y, 2), jnp.where(k == 1, flip(y, 1), jnp.where(k == 2, flip(y, 3), y)))
        even = lax.rem(j, 2) == 0
        za = jnp.where(even, flip(z, 2), flip(z, 3))
        zb = jnp.where(even, flip(z, 1), z)
        ca = pl.ds(al((yy * 4 + za) * 128, 128), 128)
        cb = pl.ds(al((yy * 4 + zb) * 128, 128), 128)
        bh = jnp.concatenate([fh[:, ca], fh[:, cb]], axis=1)
        bl = jnp.concatenate([fl[:, ca], fl[:, cb]], axis=1)
        block = mm3(oh[...], ol[...], bh, bl)
        cpart[j, 0] = block[:, :128]
        cpart[j, 1] = block[:, 128:]
        core_copy(j).start()
        return carry

    where = {}
    for j in range(8):
        for t, ez in enumerate((2, 1) if j % 2 == 0 else (3, 0)):
            where[(2, 1, 3, 0)[j // 2], ez] = (j, t)

    turns = ((1, 3), (3, 1))

    def over(p, stage):
        return (lambda e: to_z(flip(z, e))) if (p < 2) == (stage == 1) else (lambda e: to_y(flip(y, e)))

    def block_of(p, along, across):
        j, t = where[(across, along) if p < 2 else (along, across)]
        return crecv[j, t, 64 * p : 64 * p + 64, :]

    c_in = []

    def cos_join(j):
        core_copy(j).wait_recv()
        crecv[j] = crecv[j] + cpart[j, :, mine]
        for (ey, ez), (jj, t) in where.items():
            if jj != j:
                continue
            for p in range(4):
                along, across = (ez, ey) if p < 2 else (ey, ez)
                near = turns[p % 2][0]
                if along in (near, 2):
                    c_in.append(send(
                        crecv.at[j, t, 64 * p : 64 * p + 64], c1.at[p, int(along == 2), across], over(p, 1)(near)))

    def take(copies):
        for cp in copies:
            cp.wait_recv()
        del copies[:]

    def c_1b():
        take(c_in)
        for p in range(4):
            far = turns[p % 2][1]
            for n in range(4):
                s1[p, n] = block_of(p, far, n) + c1[p, 1, n]
            c_in.append(send(s1.at[p], t1.at[p], over(p, 1)(far)))

    def c_2a():
        take(c_in)
        for p in range(4):
            for n in range(4):
                o1[p, n] = (block_of(p, 0, n) + c1[p, 0, n]) + t1[p, n]
            near = turns[p % 2][0]
            lo = 1 if near == 1 else 2
            c_in.append(send(o1.at[p, lo : lo + 2], u2.at[p], over(p, 2)(near)))

    def c_2b():
        take(c_in)
        for p in range(4):
            near, far = turns[p % 2]
            s2[p] = o1[p, far] + u2[p, 1 if near == 1 else 0]
            c_in.append(send(s2.at[p], w2.at[p], over(p, 2)(far)))

    def c_end():
        take(c_in)
        for p in range(4):
            near = turns[p % 2][0]
            rows = pl.ds(al(core * 256 + 64 * p, 64), 64)
            cfin[rows, :] = (o1[p, 0] + u2[p, 0 if near == 1 else 1]) + w2[p]
        return send(cfin.at[mine], cfin.at[mine], to_core())

    lax.fori_loop(0, 2, cos_step, 0)
    next(ar_m)
    lax.fori_loop(2, 6, cos_step, 0)
    next(ar_m)
    cos_join(0)
    cos_join(1)
    lax.fori_loop(6, 8, cos_step, 0)
    next(ar_m)
    for cp in pcopies:
        cp.wait_recv()
    own = pl.ds(al(x * 256, 256), 256)
    rows_sum = (part[own, :] + precv[0]) + (precv[1] + precv[2])
    sbuf[own, :] = rows_sum
    gram = exact(rows_sum.T, rows_sum)
    g_part[0:256, :] = gram[:, :128]
    g_part[256:512, :] = gram[:, 128:]
    ar_g = all_reduce_late(g_part, g_r1, g_h2, g_r2, g_sw, g_swr, g_r3, g_fin)
    cos_join(2)
    cos_join(3)
    next(ar_m)
    next(ar_g)
    cos_join(4)
    cos_join(5)
    next(ar_m)
    scopies = [send(sbuf.at[own], sbuf.at[own], to_x(plus(x, d))) for d in (1, 2, 3)]
    cos_join(6)
    cos_join(7)
    next(ar_m)
    next(ar_g)
    next(ar_m)
    mixed = m_fin[...]
    mixed_t = mixed.T
    normal = exact(mixed_t, mixed)

    def factor_first(a, between):
        up, lo = eliminate(a[:128, :128], between)
        off = exact(lo, a[:128, 128:])
        return up, lo, off, a[128:, 128:] - exact(off.T, off)

    def factor_second(up, lo, off, rest, between):
        up2, lo2 = eliminate(rest, between)
        corner = -exact(lo2, exact(off.T, lo))
        zero = jnp.zeros((128, 128), F32)
        left = jnp.concatenate([lo, corner], axis=0)
        right = jnp.concatenate([zero, lo2], axis=0)
        inv = jnp.concatenate([left, right], axis=1)
        top = jnp.concatenate([up, off], axis=1)
        bottom = jnp.concatenate([zero, up2], axis=1)
        return inv, jnp.concatenate([top, bottom], axis=0)

    def queue(*steps):
        steps = list(steps)

        def run():
            if steps:
                steps.pop(0)()

        return run

    def step_g():
        next(ar_g)

    def rest():
        pass

    c_1b()
    first = factor_first(normal, queue(rest, step_g, step_g, c_2a))
    inverse, unused = factor_second(*first, queue(step_g, rest, c_2b, step_g))
    solve = exact(inverse.T, exact(inverse, mixed_t))
    cc = c_end()
    cc.wait_recv()
    block = exact(solve, cfin[...])
    half = al(core * 128, 128)
    jbuf[...] = block
    ra = pl.ds(half, 64)
    rb = pl.ds(al(half + 64, 64), 64)
    xbuf[y, z, ra] = jbuf[ra, :]
    xbuf[y, z, rb] = jbuf[rb, :]
    x1 = []
    for d in (1, 2, 3):
        x1.append(send(xbuf.at[y, z, ra], xbuf.at[y, z, ra], to_z(plus(z, d))))
        x1.append(send(xbuf.at[y, z, rb], xbuf.at[y, z, rb], to_y(plus(y, d))))
    next(ar_g)
    for cp in scopies:
        cp.wait_recv()
    gram = jnp.concatenate([g_fin[0:256, :], g_fin[256:512, :]], axis=1)

    forward = []

    def lot(p, e):
        rows = pl.ds(al(half + 32 * p, 32), 32)
        return xbuf.at[flip(y, e), :, rows] if p < 2 else xbuf.at[:, flip(z, e), rows]

    def x_2a():
        take(x1)
        for p in range(4):
            x1.append(send(lot(p, 0), lot(p, 0), over(p, 2)(turns[p % 2][1])))
        for p in range(4):
            forward.append(send(lot(p, 0), lot(p, 0), to_core()))

    x_last = []

    def x_2b():
        for p in range(4):
            near = turns[p % 2][0]
            x_last.append(send(lot(p, 0), lot(p, 0), over(p, 2)(near)))
        take(x1)
        for p in range(4):
            near, far = turns[p % 2]
            x_last.append(send(lot(p, far), lot(p, far), over(p, 2)(near)))
        for p in range(4):
            far = turns[p % 2][1]
            forward.append(send(lot(p, far), lot(p, far), to_core()))

    def x_end(part):
        for p in range(4):
            near, far = turns[p % 2]
            x_last[4 * part + p].wait_recv()
            e = near if part == 0 else 2
            forward.append(send(lot(p, e), lot(p, e), to_core()))

    first = factor_first(gram, queue(rest, rest, x_2a))
    inverse, upper = factor_second(*first, queue(x_2b, rest, rest, lambda: x_end(0)))
    x_end(1)
    j_out[...] = inverse
    r_out[...] = upper
    for cp in forward:
        cp.wait_recv()
    for cp in sent:
        cp.wait_send()

    def drain(j, carry):
        core_copy(j).wait_send()
        return carry

    lax.fori_loop(0, 8, drain, 0)


def last(scale, field, s, xb, inv, up, left, right, residual, sh, sl, ih, il, uh, ul):
    @pl.when(pl.program_id(0) == 0)
    def _():
        high, low = halves(s[...])
        sh[...] = high
        sl[...] = low
        high, low = halves(inv[...].T)
        ih[...] = high
        il[...] = low
        high, low = halves(up[...])
        uh[...] = high
        ul[...] = low

    j = pl.program_id(0)
    cols = pl.ds(pl.multiple_of(j * 256, 256), 256)
    row, first = j // 2, lax.rem(j, 2) * 2
    block = jnp.concatenate([xb[row, first], xb[row, first + 1]], axis=1)
    xh, xl = halves(block)
    residual[...] = field[:, cols] - mm3(sh[...], sl[...], xh, xl)
    right[...] = mm3(uh[...], ul[...], xh, xl)
    rows = pl.ds(pl.multiple_of(j * 128, 128), 128)
    left[...] = mm3(sh[rows, :], sl[rows, :], ih[...], il[...]) * scale


def per_device(cells, field, range_test, corange_test):
    def vm(*shape, dtype=F32):
        return pltpu.VMEM(shape, dtype)

    def reduce_buffers(w):
        return [
            vm(512, w), vm(256, w), vm(256, w), vm(2, 3, 32, w), vm(2, 32, w),
            vm(2, 3, 8, w), vm(4, 16, w), vm(512, w),
        ]

    any_space = pl.BlockSpec(memory_space=pl.ANY)
    here = pl.BlockSpec(memory_space=pltpu.VMEM)
    copy, s, xb, inv, up = pl.pallas_call(
        kernel,
        out_shape=(vm(1024, 2048), vm(1024, 256), vm(4, 4, 256, 128), vm(256, 256), vm(256, 256)),
        in_specs=[any_space] * 3,
        out_specs=[here] * 5,
        scratch_shapes=[
            vm(2048, 256), vm(512, 1024),
            vm(1024, 2048, dtype=BF16), vm(1024, 2048, dtype=BF16),
            vm(2048, 256, dtype=BF16), vm(2048, 256, dtype=BF16),
            vm(512, 1024, dtype=BF16), vm(512, 1024, dtype=BF16),
            vm(1024, 256), vm(3, 256, 256),
            vm(8, 2, 512, 128), vm(8, 2, 256, 128),
            vm(4, 2, 4, 64, 128), vm(4, 4, 64, 128), vm(4, 4, 64, 128), vm(4, 4, 64, 128),
            vm(4, 2, 64, 128), vm(4, 64, 128), vm(4, 64, 128), vm(512, 128),
            *reduce_buffers(256),
            vm(512, 128), vm(2, 3, 64, 128), vm(2, 64, 128), vm(2, 3, 16, 128),
            vm(32, 128), vm(32, 128), vm(4, 32, 128), vm(512, 128),
            vm(256, 128),
            pltpu.SemaphoreType.DMA((6,)),
            pltpu.SemaphoreType.DMA((180,)),
            pltpu.SemaphoreType.DMA((180,)),
            pltpu.SemaphoreType.DMA((8,)),
            pltpu.SemaphoreType.DMA((8,)),
        ],
        compiler_params=pltpu.CompilerParams(
            collective_id=0, has_side_effects=True, vmem_limit_bytes=44 * 1024 * 1024),
        name="sketch",
    )(field, range_test, corange_test)
    return pl.pallas_call(
        functools.partial(last, float(cells) ** 0.5),
        grid=(8,),
        out_shape=(
            jax.ShapeDtypeStruct((1024, 256), F32),
            jax.ShapeDtypeStruct((256, 2048), F32),
            jax.ShapeDtypeStruct((1024, 2048), F32),
        ),
        in_specs=[here] * 5,
        out_specs=(
            pl.BlockSpec((128, 256), lambda j: (j, 0)),
            pl.BlockSpec((256, 256), lambda j: (0, j)),
            pl.BlockSpec((1024, 256), lambda j: (0, j)),
        ),
        scratch_shapes=[vm(1024, 256, dtype=BF16)] * 2 + [vm(256, 256, dtype=BF16)] * 4,
        compiler_params=pltpu.CompilerParams(vmem_limit_bytes=32 * 1024 * 1024),
        name="finish",
    )(copy, s, xb, inv, up)


def solution(mesh):
    cells = 1024 * mesh.shape["space"]
    return jax.shard_map(
        functools.partial(per_device, cells),
        mesh=mesh,
        in_specs=(P("space", "tm"), P("tm", None), P(None, "space")),
        out_specs=(P("space", None), P(None, "tm"), P("space", "tm")),
        check_vma=False,
    )
```
